256 devices in a mesh: grp: 8 (over y, x_lo), lay: 32 (over x_hi, z, core).
Axes of the slice: x: 4 (x_hi: 2, x_lo: 2; x = x_hi * 2 + x_lo), y: 4, z: 8, core: 2. Of those that a mesh axis runs over, the one named last changes fastest.
Arguments:
- stored_grads: bfloat16 [8192, 32, 1024], P(('grp', 'lay'))
- inverse_fisher: float32 [32, 1024, 1024], P('lay')
- query_grads: bfloat16 [1024, 32, 1024], P('grp', 'lay'), may hold values from -6 to 6
- example_row: int32 [8, 1024], P('grp'), may hold values from 0 to 1023, each once within a row
- query_slot: int32 [1024], replicated, may hold values from 0 to 1023, each once
Outputs:
- scores: float32 [8192, 1024], P(('grp', 'lay'))
The draws below stay inside these ranges and needn't reach their ends.
All inputs are finite; a program needn't handle non-finite values.
Results may differ from the reference program's by a relative error of at most 0.0029.
Values may be sent and summed in bfloat16 or wider, within the bound.
A program may use at most 64 MiB of HBM per device.

```python
import jax
import jax.numpy as jnp
from jax import lax

K = 1024
LAYERS = 32
GROUPS = 8
EX_GRP = 1024
EXAMPLES = 8192
QUERIES = 1024


def draw_stored_grads(key, part):
    first, second = jax.random.split(jax.random.fold_in(key, 11), 2)
    base = jax.random.normal(first, (EXAMPLES, LAYERS, K), jnp.float32)
    logscale = jax.random.uniform(second, (EXAMPLES, LAYERS, 1), jnp.float32, jnp.log(0.3), jnp.log(3.0))
    return (base * jnp.exp(logscale)).astype(jnp.bfloat16)


def draw_inverse_fisher(key, part):
    first, second = jax.random.split(jax.random.fold_in(key, 23))
    noise = jax.random.normal(first, (LAYERS, K, K), jnp.float32) * (0.6 / jnp.sqrt(jnp.float32(2 * K)))
    sym = noise + jnp.swapaxes(noise, 1, 2)
    diag = jnp.exp(jax.random.uniform(second, (LAYERS, K), jnp.float32, jnp.log(0.5), jnp.log(2.0)))
    return sym + diag[:, :, None] * jnp.eye(K, dtype=jnp.float32)[None]


def level_of(rng, extent, shards, smallest, largest):
    loudness, own = 1.0, jax.random.fold_in(rng, 6)
    for axis_at, parts in shards:
        heights = jnp.exp(jax.random.uniform(jax.random.fold_in(own, axis_at), (parts,), jnp.float32, smallest / len(shards), largest / len(shards)))
        loudness = loudness * jnp.repeat(heights, extent[axis_at] // parts).reshape([-1 if axis == axis_at else 1 for axis in range(len(extent))])
    return loudness


def scatter_about(key, shape, deviation, reach, shards=(), kind=jnp.bfloat16):
    array = jax.random.normal(key, shape, jnp.float32) * deviation
    if len(shards) > 0:
        array = level_of(key, shape, shards, -0.22, 0.18) * array
    return jnp.clip(array, min=-reach, max=reach).astype(kind)


def setup_inputs(seed: int = 0) -> dict:
    arg_keys = jax.random.split(jax.random.key(seed), 6)
    stored_grads = draw_stored_grads(jax.random.fold_in(arg_keys[5], 71), 0)
    inverse_fisher = draw_inverse_fisher(jax.random.fold_in(arg_keys[5], 71), 0)
    query_grads = scatter_about(arg_keys[2], (QUERIES, LAYERS, K), 1.0, 6.0, ((0, 8), (1, 32)))
    example_row = jax.vmap(lambda own: jax.random.permutation(own, EX_GRP))(jax.random.split(arg_keys[3], GROUPS)).reshape((GROUPS, EX_GRP)).astype(jnp.int32)
    query_slot = jax.random.permutation(arg_keys[4], QUERIES).astype(jnp.int32)
    return dict(stored_grads=stored_grads, inverse_fisher=inverse_fisher, query_grads=query_grads, example_row=example_row, query_slot=query_slot)


EPS = 1e-06

def reference(stored_grads, inverse_fisher, query_grads, example_row, query_slot):
    offsets = (jnp.arange(GROUPS, dtype=jnp.int32) * EX_GRP)[:, None]
    rows_order = (example_row.astype(jnp.int32) + offsets).reshape(-1)
    queries = query_grads[query_slot.astype(jnp.int32)]
    grads_by_layer = jnp.swapaxes(stored_grads, 0, 1)
    queries_by_layer = jnp.swapaxes(queries, 0, 1)

    def layer_step(total, inputs):
        grads, fisher, asked = inputs
        pre = jnp.dot(grads.astype(jnp.float32), fisher, precision=lax.Precision.HIGHEST)
        mean_square = lax.optimization_barrier(jnp.mean(pre * pre, axis=1, keepdims=True)) + EPS
        normed = (pre * lax.rsqrt(mean_square)).astype(jnp.bfloat16)
        normed = normed[rows_order]
        part = lax.dot_general(normed, asked, (((1,), (1,)), ((), ())), preferred_element_type=jnp.float32)
        return (total + part, None)
    start = jnp.zeros((EXAMPLES, QUERIES), jnp.float32)
    total, unused = lax.scan(layer_step, start, (grads_by_layer, inverse_fisher, queries_by_layer))
    return total / jnp.sqrt(jnp.float32(K * LAYERS))
```

```python
import math

import jax
import jax.numpy as jnp
from jax import lax
from jax.experimental import pallas as pl
from jax.experimental.pallas import tpu as pltpu
from jax.sharding import Mesh
from jax.sharding import PartitionSpec as P

AXES = ("y", "xl", "xh", "z", "c")
SIZE = {"y": 4, "xl": 2, "xh": 2, "z": 8, "c": 2}
GRP = ("y", "xl")
LAY = ("xh", "z", "c")
EPS = 1e-06
K = 1024
ROWS = 32
BF16 = jnp.bfloat16
F32 = jnp.float32
IN_Z = [(a, b) for a in range(2) for b in range(2)]
FAR_FIRST = (4, 3, 5, 2, 6, 1, 7, 0)


def step_of(g):
    return lax.rem(jnp.where(lax.rem(g, 2) == 1, (g + 1) // 2, 8 - g // 2), 8)


def kernel(
    x_hbm, f_hbm, q_hbm, ex_ref, qs_ref, out_ref,
    x_v, f_v, fh, fl, q_all, qpt, sendbuf, grads, own, other, pick, col, acc,
    xs, xr, zs, zr,
    in_sem, q_send, q_recv, a_send, a_recv, e_send, e_recv, x_send, x_recv, z_send, z_recv,
):
    me = {a: lax.axis_index(a) for a in AXES}
    z, c, xh = me["z"], me["c"], me["xh"]

    def shifted(**off):
        return tuple(lax.rem(me[a] + off.get(a, 0), SIZE[a]) for a in AXES)

    def remote(src, dst, ssem, rsem, dev):
        return pltpu.make_async_remote_copy(
            src_ref=src, dst_ref=dst, send_sem=ssem, recv_sem=rsem,
            device_id=dev, device_id_type=pl.DeviceIdType.MESH,
        )

    load_x = pltpu.make_async_copy(x_hbm, x_v, in_sem.at[0])
    load_f = pltpu.make_async_copy(f_hbm, f_v, in_sem.at[1])
    grp_me = me["y"] * 2 + me["xl"]
    my_q = pl.ds(pl.multiple_of(grp_me * 128, 128), 128)
    load_q = pltpu.make_async_copy(q_hbm, q_all.at[my_q], in_sem.at[2])
    load_x.start()

    barrier = pltpu.get_barrier_semaphore()
    lay_peers = [(a, b, d) for a in range(2) for b in range(8) for d in range(2) if (a, b, d) != (0, 0, 0)]
    grp_peers = [(a, b) for a in range(4) for b in range(2) if (a, b) != (0, 0)]
    for a, b, d in lay_peers:
        pl.semaphore_signal(barrier, inc=1, device_id=shifted(xh=a, z=b, c=d), device_id_type=pl.DeviceIdType.MESH)
    for a, b in grp_peers:
        pl.semaphore_signal(barrier, inc=1, device_id=shifted(y=a, xl=b), device_id_type=pl.DeviceIdType.MESH)
    load_f.start()
    load_q.start()
    load_x.wait()
    pl.semaphore_wait(barrier, len(lay_peers) + len(grp_peers))

    q_out = []
    for i, (a, b) in enumerate(grp_peers):
        copy = remote(q_hbm, q_all.at[my_q], q_send.at[i], q_recv.at[i], shifted(y=a, xl=b))
        copy.start()
        q_out.append(copy)

    row_in = lax.broadcasted_iota(jnp.int32, (128, K), 0)
    col_in = lax.broadcasted_iota(jnp.int32, (128, K), 1)
    source = lax.rem(row_in, 32) * 32 + (row_in // 64) * 16 + lax.rem(row_in // 32, 2)
    base = source - col_in
    slot = pl.multiple_of(xh * 64 + c * 32, 32)

    def a_copy(g, q, sending):
        d = step_of(g)
        a, b = IN_Z[q]
        if sending:
            to = (me["y"], me["xl"], lax.rem(xh + a, 2), lax.rem(z + d, 8), lax.rem(c + b, 2))
            rows = pl.multiple_of(to[2] * 64 + to[4] * 32, 32)
            src, dst = sendbuf.at[g, pl.ds(rows, 32)], grads.at[z, pl.ds(slot, 32)]
        else:
            to = (me["y"], me["xl"], lax.rem(xh + a, 2), lax.rem(z + 8 - d, 8), lax.rem(c + b, 2))
            rows = pl.multiple_of(to[2] * 64 + to[4] * 32, 32)
            src, dst = sendbuf.at[g, pl.ds(rows, 32)], grads.at[to[3], pl.ds(rows, 32)]
        return remote(src, dst, a_send.at[g, q], a_recv.at[g, q], to)

    def prepare(g):
        to_z = lax.rem(z + step_of(g), 8)
        mask = jnp.where(base + 2 * to_z == 0, 1.0, 0.0).astype(BF16)
        sendbuf[g] = jnp.dot(mask, x_v[...], preferred_element_type=F32).astype(BF16)

    prepare(0)
    for q in range(1, 4):
        a_copy(0, q, True).start()
    grads[z, pl.ds(slot, 32)] = sendbuf[0, pl.ds(slot, 32)]

    def prepare_and_send(g, carry):
        prepare(g)
        for q in range(4):
            a_copy(g, q, True).start()
        return carry

    lax.fori_loop(1, 8, prepare_and_send, 0)

    load_f.wait()

    def split(i, carry):
        rows = pl.ds(pl.multiple_of(i * 128, 128), 128)
        f = f_v[rows, :]
        hi = f.astype(BF16)
        fh[rows, :] = hi
        fl[rows, :] = (f - hi.astype(F32)).astype(BF16)
        return carry

    lax.fori_loop(0, 8, split, 0)

    diagonal = lax.broadcasted_iota(jnp.int32, (128, 128), 0) == lax.broadcasted_iota(jnp.int32, (128, 128), 1)

    def as_column(ref, i):
        lanes = pl.ds(pl.multiple_of(i * 128, 128), 128)
        row = jnp.broadcast_to(ref[:, lanes].astype(F32), (128, 128))
        return jnp.sum(jnp.where(diagonal, row, 0.0), axis=1, keepdims=True)

    def columns(i, carry):
        rows = pl.ds(pl.multiple_of(i * 128, 128), 128)
        col[rows, :] = jnp.broadcast_to(as_column(ex_ref, i), (128, 128))
        return carry

    lax.fori_loop(0, 8, columns, 0)

    lane = lax.broadcasted_iota(jnp.int32, (32, 128), 1)
    stored = ((lane // 64) * 512 + lax.rem(lane, 64)).astype(F32)

    def picks(i, carry):
        to_z, to_xh = i // 2, lax.rem(i, 2)
        wanted = col[pl.ds(pl.multiple_of(to_xh * 512 + to_z * 64 + c * 32, 32), 32), :] - stored
        rows = pl.ds(pl.multiple_of(i * 32, 32), 32)
        for zg in range(8):
            pick[zg, rows, :] = jnp.where(wanted == float(zg * 64), 1.0, 0.0).astype(BF16)
        return carry

    lax.fori_loop(0, 16, picks, 0)
    acc[...] = jnp.zeros_like(acc)

    load_q.wait()
    for i, (a, b) in enumerate(grp_peers):
        src = shifted(y=4 - a, xl=2 - b)
        rows = pl.ds(pl.multiple_of((src[0] * 2 + src[1]) * 128, 128), 128)
        remote(q_hbm, q_all.at[rows], q_send.at[i], q_recv.at[i], src).wait_recv()
    lanes_f = lax.broadcasted_iota(jnp.int32, (128, K), 1).astype(F32)

    def ask(i, carry):
        mask = jnp.where(as_column(qs_ref, i) == lanes_f, 1.0, 0.0).astype(BF16)
        chosen = jnp.dot(mask, q_all[...], preferred_element_type=F32)
        lanes = pl.ds(pl.multiple_of(i * 128, 128), 128)
        qpt[:, lanes] = jnp.transpose(chosen).astype(BF16)
        return carry

    lax.fori_loop(0, 8, ask, 0)

    def source_z(g):
        return lax.rem(z + 8 - step_of(g), 8)

    def exchange(g):
        at = source_z(g)
        return remote(own.at[at], other.at[at], e_send.at[g], e_recv.at[g], shifted(c=1))

    def score(g, count):
        for q in range(4 - count, 4):
            a_copy(g, q, False).wait_recv()
        at = source_z(g)
        rows = grads[at]
        pre = jnp.dot(rows, fh[...], preferred_element_type=F32) + jnp.dot(rows, fl[...], preferred_element_type=F32)
        mean_square = jnp.mean(pre * pre, axis=1, keepdims=True) + EPS
        normed = (pre * lax.rsqrt(mean_square)).astype(BF16)
        own[at] = jnp.dot(normed, qpt[...], preferred_element_type=F32)
        exchange(g).start()

    def collect(g):
        exchange(g).wait_recv()
        at = source_z(g)
        both = (own[at] + other[at]).astype(BF16)
        acc[...] += jnp.dot(pick[at], both, preferred_element_type=F32)

    score(0, 3)

    def score_and_collect(g, carry):
        score(g, 4)
        collect(g - 1)
        return carry

    lax.fori_loop(1, 8, score_and_collect, 0)
    collect(7)

    def piece(k, to_xh):
        to_z = lax.rem(z + FAR_FIRST[k], 8)
        return acc[pl.ds(pl.multiple_of(to_z * 64 + to_xh * 32, 32), 32), :]

    def x_copy(k):
        return remote(xs.at[k], xr.at[k], x_send.at[k], x_recv.at[k], shifted(xh=1))

    def z_copy(k):
        return remote(zs.at[k], zr.at[k], z_send.at[k], z_recv.at[k], shifted(z=FAR_FIRST[k]))

    for k in range(8):
        xs[k] = piece(k, 1 - xh).astype(BF16)
        x_copy(k).start()
    for k in range(7):
        x_copy(k).wait_recv()
        zs[k] = (piece(k, xh) + xr[k].astype(F32)).astype(BF16)
        z_copy(k).start()
    x_copy(7).wait_recv()
    total = piece(7, xh) + xr[7].astype(F32)
    for k in range(6, -1, -1):
        z_copy(k).wait_recv()
        total = total + zr[k].astype(F32)
    out_ref[...] = total * (1.0 / math.sqrt(K * 32))

    for copy in q_out:
        copy.wait_send()
    for q in range(1, 4):
        a_copy(0, q, True).wait_send()

    def drain(g, carry):
        for q in range(4):
            a_copy(g, q, True).wait_send()
        exchange(g).wait_send()
        return carry

    lax.fori_loop(1, 8, drain, 0)
    exchange(0).wait_send()
    for k in range(8):
        x_copy(k).wait_send()
        if k < 7:
            z_copy(k).wait_send()


def body(stored_grads, inverse_fisher, query_grads, example_row, query_slot):
    dma = pltpu.SemaphoreType.DMA
    hbm = pl.BlockSpec(memory_space=pl.ANY)
    vmem = pl.BlockSpec(memory_space=pltpu.VMEM)
    return pl.pallas_call(
        kernel,
        out_shape=jax.ShapeDtypeStruct((ROWS, K), F32),
        in_specs=[hbm, hbm, hbm, vmem, vmem],
        out_specs=vmem,
        scratch_shapes=[
            pltpu.VMEM((K, K), BF16),
            pltpu.VMEM((K, K), F32),
            pltpu.VMEM((K, K), BF16),
            pltpu.VMEM((K, K), BF16),
            pltpu.VMEM((K, K), BF16),
            pltpu.VMEM((K, K), BF16),
            pltpu.VMEM((8, 128, K), BF16),
            pltpu.VMEM((8, 128, K), BF16),
            pltpu.VMEM((8, 128, K), F32),
            pltpu.VMEM((8, 128, K), F32),
            pltpu.VMEM((8, 512, 128), BF16),
            pltpu.VMEM((K, 128), F32),
            pltpu.VMEM((512, K), F32),
            pltpu.VMEM((8, ROWS, K), BF16),
            pltpu.VMEM((8, ROWS, K), BF16),
            pltpu.VMEM((8, ROWS, K), BF16),
            pltpu.VMEM((8, ROWS, K), BF16),
            dma((3,)), dma((7,)), dma((7,)), dma((8, 4)), dma((8, 4)), dma((8,)), dma((8,)),
            dma((8,)), dma((8,)), dma((8,)), dma((8,)),
        ],
        name="attribution",
        compiler_params=pltpu.CompilerParams(
            collective_id=0, has_side_effects=True, vmem_limit_bytes=60 * 1024 * 1024
        ),
    )(
        stored_grads.reshape(K, K),
        inverse_fisher.reshape(K, K),
        query_grads.reshape(128, K),
        example_row,
        query_slot.reshape(1, K),
    )


def solution(mesh):
    split = Mesh(mesh.devices.reshape(tuple(SIZE[a] for a in AXES)), AXES)
    placed = (P(AXES, None, None), P(LAY, None, None), P(GRP, LAY, None), P(GRP, None), P())
    return jax.shard_map(body, mesh=split, in_specs=placed, out_specs=P(AXES, None), check_vma=False)
```

```python
import math

import jax
import jax.numpy as jnp
from jax import lax
from jax.experimental import pallas as pl
from jax.experimental.pallas import tpu as pltpu
from jax.sharding import Mesh
from jax.sharding import PartitionSpec as P

AXES = ("y", "xl", "xh", "z", "c")
SIZE = {"y": 4, "xl": 2, "xh": 2, "z": 8, "c": 2}
GRP = ("y", "xl")
LAY = ("xh", "z", "c")
EPS = 1e-06
K = 1024
ROWS = 32
BF16 = jnp.bfloat16
F32 = jnp.float32
IN_Z = [(a, b) for a in range(2) for b in range(2)]
EARLY = 3
AHEAD = 4
FAR_FIRST = (4, 3, 5, 2, 6, 1, 7, 0)


def step_of(g):
    return jnp.where(lax.rem(g, 2) == 1, (g + 7) // 2, lax.rem((8 - g) // 2, 4))


def kernel(
    x_hbm, f_hbm, q_hbm, ex_ref, qs_ref, out_ref,
    x_v, f_v, fh, fl, q_all, qpt, sendbuf, grads, normed, own, other, pick, col, acc,
    xs, xr, zs, zr,
    in_sem, q_send, q_recv, a_send, a_recv, e_send, e_recv, x_send, x_recv, z_send, z_recv,
):
    me = {a: lax.axis_index(a) for a in AXES}
    z, c, xh = me["z"], me["c"], me["xh"]

    def shifted(**off):
        return tuple(lax.rem(me[a] + off.get(a, 0), SIZE[a]) for a in AXES)

    def remote(src, dst, ssem, rsem, dev):
        return pltpu.make_async_remote_copy(
            src_ref=src, dst_ref=dst, send_sem=ssem, recv_sem=rsem,
            device_id=dev, device_id_type=pl.DeviceIdType.MESH,
        )

    load_x = pltpu.make_async_copy(x_hbm, x_v, in_sem.at[0])
    load_f = pltpu.make_async_copy(f_hbm, f_v, in_sem.at[1])
    grp_me = me["y"] * 2 + me["xl"]
    my_q = pl.ds(pl.multiple_of(grp_me * 128, 128), 128)
    load_q = pltpu.make_async_copy(q_hbm, q_all.at[my_q], in_sem.at[2])
    load_x.start()

    barrier = pltpu.get_barrier_semaphore()
    lay_peers = [(a, b, d) for a in range(2) for b in range(8) for d in range(2) if (a, b, d) != (0, 0, 0)]
    grp_peers = [(0, 1), (1, 0), (2, 0), (3, 0)]
    for a, b, d in lay_peers:
        pl.semaphore_signal(barrier, inc=1, device_id=shifted(xh=a, z=b, c=d), device_id_type=pl.DeviceIdType.MESH)
    for a, b in grp_peers:
        pl.semaphore_signal(barrier, inc=1, device_id=shifted(y=a, xl=b), device_id_type=pl.DeviceIdType.MESH)
    load_f.start()
    load_q.start()
    row_in = lax.broadcasted_iota(jnp.int32, (128, K), 0)
    col_in = lax.broadcasted_iota(jnp.int32, (128, K), 1)
    source = lax.rem(row_in, 32) * 32 + (row_in // 64) * 16 + lax.rem(row_in // 32, 2)
    base = source - col_in
    slot = pl.multiple_of(xh * 64 + c * 32, 32)

    def a_copy(g, q, sending):
        d = step_of(g)
        a, b = IN_Z[q]
        if sending:
            to = (me["y"], me["xl"], lax.rem(xh + a, 2), lax.rem(z + d, 8), lax.rem(c + b, 2))
            rows = pl.multiple_of(to[2] * 64 + to[4] * 32, 32)
            src, dst = sendbuf.at[g, pl.ds(rows, 32)], grads.at[z, pl.ds(slot, 32)]
        else:
            to = (me["y"], me["xl"], lax.rem(xh + a, 2), lax.rem(z + 8 - d, 8), lax.rem(c + b, 2))
            rows = pl.multiple_of(to[2] * 64 + to[4] * 32, 32)
            src, dst = sendbuf.at[g, pl.ds(rows, 32)], grads.at[to[3], pl.ds(rows, 32)]
        return remote(src, dst, a_send.at[g, q], a_recv.at[g, q], to)

    def prepare(g):
        to_z = lax.rem(z + step_of(g), 8)
        mask = jnp.where(base + 2 * to_z == 0, 1.0, 0.0).astype(BF16)
        sendbuf[g] = jnp.dot(mask, x_v[...], preferred_element_type=F32).astype(BF16)

    def prepare_next(g, carry):
        prepare(g)
        return carry

    def send(g):
        for q in range(4):
            a_copy(g, q, True).start()

    def prepare_and_send(g, carry):
        prepare(g)
        send(g)
        return carry

    load_x.wait()
    lax.fori_loop(0, 2, prepare_next, 0)
    pl.semaphore_wait(barrier, len(lay_peers) + len(grp_peers))

    def q_rows(y, xl):
        return pl.ds(pl.multiple_of((y * 2 + xl) * 128, 128), 128)

    def q_copy(i, sending):
        a = 0 if i == 0 else (i - 1) % 3 + 1
        b = 1 if i == 0 else 0
        if sending:
            rows = q_rows(me["y"], me["xl"] if i < 4 else 1 - me["xl"])
            src = q_hbm if i < 4 else q_all.at[rows]
            to = shifted(y=a, xl=b)
        else:
            to = shifted(y=4 - a, xl=b)
            rows = q_rows(to[0], to[1] if i < 4 else 1 - to[1])
            src = q_hbm
        return remote(src, q_all.at[rows], q_send.at[i], q_recv.at[i], to)

    for i in range(4):
        q_copy(i, True).start()
    send(1)
    for q in range(1, 4):
        a_copy(0, q, True).start()
    lax.fori_loop(2, AHEAD + 1, prepare_and_send, 0)
    lax.fori_loop(AHEAD + 1, 8, prepare_next, 0)
    grads[z, pl.ds(slot, 32)] = sendbuf[0, pl.ds(slot, 32)]

    load_f.wait()

    def split(i, carry):
        rows = pl.ds(pl.multiple_of(i * 128, 128), 128)
        f = f_v[rows, :]
        hi = f.astype(BF16)
        fh[rows, :] = hi
        fl[rows, :] = (f - hi.astype(F32)).astype(BF16)
        return carry

    lax.fori_loop(0, 8, split, 0)

    q_copy(0, False).wait_recv()
    for i in range(4, 7):
        q_copy(i, True).start()

    diagonal = lax.broadcasted_iota(jnp.int32, (128, 128), 0) == lax.broadcasted_iota(jnp.int32, (128, 128), 1)

    def as_column(ref, i):
        lanes = pl.ds(pl.multiple_of(i * 128, 128), 128)
        row = jnp.broadcast_to(ref[:, lanes].astype(F32), (128, 128))
        return jnp.sum(jnp.where(diagonal, row, 0.0), axis=1, keepdims=True)

    def columns(i, carry):
        rows = pl.ds(pl.multiple_of(i * 128, 128), 128)
        col[rows, :] = jnp.broadcast_to(as_column(ex_ref, i), (128, 128))
        return carry

    lax.fori_loop(0, 8, columns, 0)

    lane = lax.broadcasted_iota(jnp.int32, (32, 128), 1)
    stored = ((lane // 64) * 512 + lax.rem(lane, 64)).astype(F32)

    def picks(i, carry):
        to_z, to_xh = i // 2, lax.rem(i, 2)
        wanted = col[pl.ds(pl.multiple_of(to_xh * 512 + to_z * 64 + c * 32, 32), 32), :] - stored
        rows = pl.ds(pl.multiple_of(i * 32, 32), 32)
        for zg in range(8):
            pick[zg, rows, :] = jnp.where(wanted == float(zg * 64), 1.0, 0.0).astype(BF16)
        return carry

    lax.fori_loop(0, 16, picks, 0)
    acc[...] = jnp.zeros_like(acc)

    def source_z(g):
        return lax.rem(z + 8 - step_of(g), 8)

    def arrived(g):
        for q in range(4):
            a_copy(g, q, True).wait_send()

        @pl.when(g + AHEAD < 8)
        def _():
            send(g + AHEAD)

        for q in range(4):
            a_copy(g, q, False).wait_recv()

    def normalise(g):
        at = source_z(g)
        rows = grads[at]
        pre = jnp.dot(rows, fh[...], preferred_element_type=F32) + jnp.dot(rows, fl[...], preferred_element_type=F32)
        mean_square = jnp.mean(pre * pre, axis=1, keepdims=True) + EPS
        normed[at] = (pre * lax.rsqrt(mean_square)).astype(BF16)

    def normalise_next(g, carry):
        arrived(g)
        normalise(g)
        return carry

    for q in range(1, 4):
        a_copy(0, q, False).wait_recv()
    normalise(0)
    lax.fori_loop(1, EARLY, normalise_next, 0)

    load_q.wait()
    for i in range(1, 7):
        q_copy(i, False).wait_recv()
    lanes_f = lax.broadcasted_iota(jnp.int32, (128, K), 1).astype(F32)

    def ask(i, carry):
        mask = jnp.where(as_column(qs_ref, i) == lanes_f, 1.0, 0.0).astype(BF16)
        chosen = jnp.dot(mask, q_all[...], preferred_element_type=F32)
        lanes = pl.ds(pl.multiple_of(i * 128, 128), 128)
        qpt[:, lanes] = jnp.transpose(chosen).astype(BF16)
        return carry

    lax.fori_loop(0, 8, ask, 0)

    def exchange(g):
        at = source_z(g)
        return remote(own.at[at], other.at[at], e_send.at[g], e_recv.at[g], shifted(c=1))

    def score(g):
        at = source_z(g)
        own[at] = jnp.dot(normed[at], qpt[...], preferred_element_type=F32)
        exchange(g).start()

    def collect(g):
        exchange(g).wait_recv()
        at = source_z(g)
        both = (own[at] + other[at]).astype(BF16)
        acc[...] += jnp.dot(pick[at], both, preferred_element_type=F32)

    score(0)

    def score_early(g, carry):
        score(g)
        collect(g - 1)
        return carry

    lax.fori_loop(1, EARLY, score_early, 0)

    def score_late(g, carry):
        arrived(g)
        normalise(g)
        score(g)
        collect(g - 1)
        return carry

    lax.fori_loop(EARLY, 8, score_late, 0)
    collect(7)

    def piece(k, to_xh):
        to_z = lax.rem(z + FAR_FIRST[k], 8)
        return acc[pl.ds(pl.multiple_of(to_z * 64 + to_xh * 32, 32), 32), :]

    def x_copy(k):
        return remote(xs.at[k], xr.at[k], x_send.at[k], x_recv.at[k], shifted(xh=1))

    def z_copy(k):
        return remote(zs.at[k], zr.at[k], z_send.at[k], z_recv.at[k], shifted(z=FAR_FIRST[k]))

    for k in range(8):
        xs[k] = piece(k, 1 - xh).astype(BF16)
        x_copy(k).start()
    for k in range(7):
        x_copy(k).wait_recv()
        zs[k] = (piece(k, xh) + xr[k].astype(F32)).astype(BF16)
        z_copy(k).start()
    x_copy(7).wait_recv()
    total = piece(7, xh) + xr[7].astype(F32)
    for k in range(6, -1, -1):
        z_copy(k).wait_recv()
        total = total + zr[k].astype(F32)
    out_ref[...] = total * (1.0 / math.sqrt(K * 32))

    for i in range(7):
        q_copy(i, True).wait_send()
    for q in range(1, 4):
        a_copy(0, q, True).wait_send()

    def drain(g, carry):
        exchange(g).wait_send()
        return carry

    lax.fori_loop(1, 8, drain, 0)
    exchange(0).wait_send()
    for k in range(8):
        x_copy(k).wait_send()
        if k < 7:
            z_copy(k).wait_send()


def body(stored_grads, inverse_fisher, query_grads, example_row, query_slot):
    dma = pltpu.SemaphoreType.DMA
    hbm = pl.BlockSpec(memory_space=pl.ANY)
    vmem = pl.BlockSpec(memory_space=pltpu.VMEM)
    return pl.pallas_call(
        kernel,
        out_shape=jax.ShapeDtypeStruct((ROWS, K), F32),
        in_specs=[hbm, hbm, hbm, vmem, vmem],
        out_specs=vmem,
        scratch_shapes=[
            pltpu.VMEM((K, K), BF16),
            pltpu.VMEM((K, K), F32),
            pltpu.VMEM((K, K), BF16),
            pltpu.VMEM((K, K), BF16),
            pltpu.VMEM((K, K), BF16),
            pltpu.VMEM((K, K), BF16),
            pltpu.VMEM((8, 128, K), BF16),
            pltpu.VMEM((8, 128, K), BF16),
            pltpu.VMEM((8, 128, K), BF16),
            pltpu.VMEM((8, 128, K), F32),
            pltpu.VMEM((8, 128, K), F32),
            pltpu.VMEM((8, 512, 128), BF16),
            pltpu.VMEM((K, 128), F32),
            pltpu.VMEM((512, K), F32),
            pltpu.VMEM((8, ROWS, K), BF16),
            pltpu.VMEM((8, ROWS, K), BF16),
            pltpu.VMEM((8, ROWS, K), BF16),
            pltpu.VMEM((8, ROWS, K), BF16),
            dma((3,)), dma((7,)), dma((7,)), dma((8, 4)), dma((8, 4)), dma((8,)), dma((8,)),
            dma((8,)), dma((8,)), dma((8,)), dma((8,)),
        ],
        name="attribution",
        compiler_params=pltpu.CompilerParams(
            collective_id=0, has_side_effects=True, vmem_limit_bytes=60 * 1024 * 1024
        ),
    )(
        stored_grads.reshape(K, K),
        inverse_fisher.reshape(K, K),
        query_grads.reshape(128, K),
        example_row,
        query_slot.reshape(1, K),
    )


def solution(mesh):
    split = Mesh(mesh.devices.reshape(tuple(SIZE[a] for a in AXES)), AXES)
    placed = (P(AXES, None, None), P(LAY, None, None), P(GRP, LAY, None), P(GRP, None), P())
    return jax.shard_map(body, mesh=split, in_specs=placed, out_specs=P(AXES, None), check_vma=False)
```

```python
import math

import jax
import jax.numpy as jnp
from jax import lax
from jax.experimental import pallas as pl
from jax.experimental.pallas import tpu as pltpu
from jax.sharding import Mesh
from jax.sharding import PartitionSpec as P

AXES = ("y", "xl", "xh", "z", "c")
SIZE = {"y": 4, "xl": 2, "xh": 2, "z": 8, "c": 2}
GRP = ("y", "xl")
LAY = ("xh", "z", "c")
EPS = 1e-06
K = 1024
ROWS = 32
BF16 = jnp.bfloat16
F32 = jnp.float32
IN_Z = [(a, b) for a in range(2) for b in range(2)]
EARLY = 3
AHEAD = 4
FAR_FIRST = (4, 3, 5, 2, 6, 1, 7, 0)


def step_of(g):
    return jnp.where(lax.rem(g, 2) == 1, (g + 7) // 2, lax.rem((8 - g) // 2, 4))


def kernel(
    x_hbm, f_hbm, q_hbm, order_ref, out_ref,
    x_v, f_v, fh, fl, q_all, qpt, sendbuf, grads, normed, own, other, pick, col, acc,
    xs, xr, zs, zr,
    in_sem, q_send, q_recv, a_send, a_recv, e_send, e_recv, x_send, x_recv, z_send, z_recv,
):
    me = {a: lax.axis_index(a) for a in AXES}
    z, c, xh = me["z"], me["c"], me["xh"]

    def shifted(**off):
        return tuple(lax.rem(me[a] + off.get(a, 0), SIZE[a]) for a in AXES)

    def remote(src, dst, ssem, rsem, dev):
        return pltpu.make_async_remote_copy(
            src_ref=src, dst_ref=dst, send_sem=ssem, recv_sem=rsem,
            device_id=dev, device_id_type=pl.DeviceIdType.MESH,
        )

    load_x = pltpu.make_async_copy(x_hbm, x_v, in_sem.at[0])
    load_f = pltpu.make_async_copy(f_hbm, f_v, in_sem.at[1])
    grp_me = me["y"] * 2 + me["xl"]
    my_q = pl.ds(pl.multiple_of(grp_me * 128, 128), 128)
    load_q = pltpu.make_async_copy(q_hbm, q_all.at[my_q], in_sem.at[2])
    load_x.start()

    barrier = pltpu.get_barrier_semaphore()
    lay_peers = [(a, b, d) for a in range(2) for b in range(8) for d in range(2) if (a, b, d) != (0, 0, 0)]
    grp_peers = [(0, 1), (1, 0), (2, 0), (3, 0)]
    lay_peers.sort(key=lambda p: -(2 * p[0] + min(p[1], 8 - p[1])))
    for a, b, d in lay_peers:
        pl.semaphore_signal(barrier, inc=1, device_id=shifted(xh=a, z=b, c=d), device_id_type=pl.DeviceIdType.MESH)
    for a, b in grp_peers:
        pl.semaphore_signal(barrier, inc=1, device_id=shifted(y=a, xl=b), device_id_type=pl.DeviceIdType.MESH)
    load_f.start()
    load_q.start()
    row_in = lax.broadcasted_iota(jnp.int32, (128, K), 0)
    col_in = lax.broadcasted_iota(jnp.int32, (128, K), 1)
    source = lax.rem(row_in, 32) * 32 + (row_in // 64) * 16 + lax.rem(row_in // 32, 2)
    base = source - col_in
    slot = pl.multiple_of(xh * 64 + c * 32, 32)

    def a_copy(g, q, sending):
        d = step_of(g)
        a, b = IN_Z[q]
        if sending:
            to = (me["y"], me["xl"], lax.rem(xh + a, 2), lax.rem(z + d, 8), lax.rem(c + b, 2))
            rows = pl.multiple_of(to[2] * 64 + to[4] * 32, 32)
            src, dst = sendbuf.at[g, pl.ds(rows, 32)], grads.at[z, pl.ds(slot, 32)]
        else:
            to = (me["y"], me["xl"], lax.rem(xh + a, 2), lax.rem(z + 8 - d, 8), lax.rem(c + b, 2))
            rows = pl.multiple_of(to[2] * 64 + to[4] * 32, 32)
            src, dst = sendbuf.at[g, pl.ds(rows, 32)], grads.at[to[3], pl.ds(rows, 32)]
        return remote(src, dst, a_send.at[g, q], a_recv.at[g, q], to)

    def prepare(g):
        to_z = lax.rem(z + step_of(g), 8)
        mask = jnp.where(base + 2 * to_z == 0, 1.0, 0.0).astype(BF16)
        sendbuf[g] = jnp.dot(mask, x_v[...], preferred_element_type=F32).astype(BF16)

    def prepare_next(g, carry):
        prepare(g)
        return carry

    def send(g):
        for q in (2, 3, 0, 1):
            a_copy(g, q, True).start()

    def prepare_and_send(g, carry):
        prepare(g)
        send(g)
        return carry

    load_x.wait()
    lax.fori_loop(0, 2, prepare_next, 0)
    pl.semaphore_wait(barrier, len(lay_peers) + len(grp_peers))

    def q_rows(y, xl):
        return pl.ds(pl.multiple_of((y * 2 + xl) * 128, 128), 128)

    def q_copy(i, sending):
        a = 0 if i == 0 else (i - 1) % 3 + 1
        b = 1 if i == 0 else 0
        if sending:
            rows = q_rows(me["y"], me["xl"] if i < 4 else 1 - me["xl"])
            src = q_hbm if i < 4 else q_all.at[rows]
            to = shifted(y=a, xl=b)
        else:
            to = shifted(y=4 - a, xl=b)
            rows = q_rows(to[0], to[1] if i < 4 else 1 - to[1])
            src = q_hbm
        return remote(src, q_all.at[rows], q_send.at[i], q_recv.at[i], to)

    for i in range(4):
        q_copy(i, True).start()
    send(1)
    for q in range(1, 4):
        a_copy(0, q, True).start()
    lax.fori_loop(2, AHEAD + 1, prepare_and_send, 0)
    lax.fori_loop(AHEAD + 1, 8, prepare_next, 0)
    grads[z, pl.ds(slot, 32)] = sendbuf[0, pl.ds(slot, 32)]

    load_f.wait()

    def split(i, carry):
        rows = pl.ds(pl.multiple_of(i * 128, 128), 128)
        f = f_v[rows, :]
        hi = f.astype(BF16)
        fh[rows, :] = hi
        fl[rows, :] = (f - hi.astype(F32)).astype(BF16)
        return carry

    lax.fori_loop(0, 8, split, 0)

    q_copy(0, False).wait_recv()
    for i in range(4, 7):
        q_copy(i, True).start()

    diagonal = lax.broadcasted_iota(jnp.int32, (128, 128), 0) == lax.broadcasted_iota(jnp.int32, (128, 128), 1)

    def as_column(which, i):
        lanes = pl.ds(pl.multiple_of(i * 128, 128), 128)
        row = jnp.broadcast_to(order_ref[pl.ds(which, 1), lanes].astype(F32), (128, 128))
        return jnp.sum(jnp.where(diagonal, row, 0.0), axis=1, keepdims=True)

    def columns(i, carry):
        rows = pl.ds(pl.multiple_of(i * 128, 128), 128)
        col[rows, :] = jnp.broadcast_to(as_column(0, i), (128, 128))
        return carry

    lax.fori_loop(0, 8, columns, 0)

    lane = lax.broadcasted_iota(jnp.int32, (32, 128), 1)
    stored = ((lane // 64) * 512 + lax.rem(lane, 64)).astype(F32)

    def picks(i, carry):
        to_z, to_xh = i // 2, lax.rem(i, 2)
        wanted = col[pl.ds(pl.multiple_of(to_xh * 512 + to_z * 64 + c * 32, 32), 32), :] - stored
        rows = pl.ds(pl.multiple_of(i * 32, 32), 32)
        for zg in range(8):
            pick[zg, rows, :] = jnp.where(wanted == float(zg * 64), 1.0, 0.0).astype(BF16)
        return carry

    lax.fori_loop(0, 16, picks, 0)
    acc[...] = jnp.zeros_like(acc)

    def source_z(g):
        return lax.rem(z + 8 - step_of(g), 8)

    def arrived(g):
        for q in range(4):
            a_copy(g, q, True).wait_send()

        @pl.when(g + AHEAD < 8)
        def _():
            send(g + AHEAD)

        for q in range(4):
            a_copy(g, q, False).wait_recv()

    def normalise(g):
        at = source_z(g)
        rows = grads[at]
        pre = jnp.dot(rows, fh[...], preferred_element_type=F32) + jnp.dot(rows, fl[...], preferred_element_type=F32)
        mean_square = jnp.mean(pre * pre, axis=1, keepdims=True) + EPS
        normed[at] = (pre * lax.rsqrt(mean_square)).astype(BF16)

    def normalise_next(g, carry):
        arrived(g)
        normalise(g)
        return carry

    for q in range(1, 4):
        a_copy(0, q, False).wait_recv()
    normalise(0)
    lax.fori_loop(1, EARLY, normalise_next, 0)

    load_q.wait()
    for i in range(1, 7):
        q_copy(i, False).wait_recv()
    lanes_f = lax.broadcasted_iota(jnp.int32, (128, K), 1).astype(F32)

    def ask(i, carry):
        mask = jnp.where(as_column(1, i) == lanes_f, 1.0, 0.0).astype(BF16)
        chosen = jnp.dot(mask, q_all[...], preferred_element_type=F32)
        lanes = pl.ds(pl.multiple_of(i * 128, 128), 128)
        qpt[:, lanes] = jnp.transpose(chosen).astype(BF16)
        return carry

    lax.fori_loop(0, 8, ask, 0)

    def exchange(g):
        at = source_z(g)
        return remote(own.at[at], other.at[at], e_send.at[g], e_recv.at[g], shifted(c=1))

    def score(g):
        at = source_z(g)
        own[at] = jnp.dot(normed[at], qpt[...], preferred_element_type=F32)
        exchange(g).start()

    def collect(g):
        exchange(g).wait_recv()
        at = source_z(g)
        both = (own[at] + other[at]).astype(BF16)
        acc[...] += jnp.dot(pick[at], both, preferred_element_type=F32)

    score(0)

    def score_early(g, carry):
        score(g)
        collect(g - 1)
        return carry

    lax.fori_loop(1, EARLY, score_early, 0)

    def score_late(g, carry):
        arrived(g)
        normalise(g)
        score(g)
        collect(g - 1)
        return carry

    lax.fori_loop(EARLY, 8, score_late, 0)
    collect(7)

    def piece(k, to_xh):
        to_z = lax.rem(z + FAR_FIRST[k], 8)
        return acc[pl.ds(pl.multiple_of(to_z * 64 + to_xh * 32, 32), 32), :]

    def x_copy(k):
        return remote(xs.at[k], xr.at[k], x_send.at[k], x_recv.at[k], shifted(xh=1))

    def z_copy(k):
        return remote(zs.at[k], zr.at[k], z_send.at[k], z_recv.at[k], shifted(z=FAR_FIRST[k]))

    for k in range(8):
        xs[k] = piece(k, 1 - xh).astype(BF16)
        x_copy(k).start()
    for k in range(7):
        x_copy(k).wait_recv()
        zs[k] = (piece(k, xh) + xr[k].astype(F32)).astype(BF16)
        z_copy(k).start()
    x_copy(7).wait_recv()
    total = piece(7, xh) + xr[7].astype(F32)
    for k in range(6, -1, -1):
        z_copy(k).wait_recv()
        total = total + zr[k].astype(F32)
    out_ref[...] = total

    for i in range(7):
        q_copy(i, True).wait_send()
    for q in range(1, 4):
        a_copy(0, q, True).wait_send()

    def drain(g, carry):
        exchange(g).wait_send()
        return carry

    lax.fori_loop(1, 8, drain, 0)
    exchange(0).wait_send()
    for k in range(8):
        x_copy(k).wait_send()
        if k < 7:
            z_copy(k).wait_send()


def body(stored_grads, inverse_fisher, query_grads, example_row, query_slot):
    dma = pltpu.SemaphoreType.DMA
    hbm = pl.BlockSpec(memory_space=pltpu.HBM)
    vmem = pl.BlockSpec(memory_space=pltpu.VMEM)
    total = pl.pallas_call(
        kernel,
        out_shape=jax.ShapeDtypeStruct((ROWS, K), F32),
        in_specs=[hbm, hbm, hbm, vmem],
        out_specs=vmem,
        scratch_shapes=[
            pltpu.VMEM((K, K), BF16),
            pltpu.VMEM((K, K), F32),
            pltpu.VMEM((K, K), BF16),
            pltpu.VMEM((K, K), BF16),
            pltpu.VMEM((K, K), BF16),
            pltpu.VMEM((K, K), BF16),
            pltpu.VMEM((8, 128, K), BF16),
            pltpu.VMEM((8, 128, K), BF16),
            pltpu.VMEM((8, 128, K), BF16),
            pltpu.VMEM((8, 128, K), F32),
            pltpu.VMEM((8, 128, K), F32),
            pltpu.VMEM((8, 512, 128), BF16),
            pltpu.VMEM((K, 128), F32),
            pltpu.VMEM((512, K), F32),
            pltpu.VMEM((8, ROWS, K), BF16),
            pltpu.VMEM((8, ROWS, K), BF16),
            pltpu.VMEM((8, ROWS, K), BF16),
            pltpu.VMEM((8, ROWS, K), BF16),
            dma((3,)), dma((7,)), dma((7,)), dma((8, 4)), dma((8, 4)), dma((8,)), dma((8,)),
            dma((8,)), dma((8,)), dma((8,)), dma((8,)),
        ],
        name="attribution",
        compiler_params=pltpu.CompilerParams(
            collective_id=0, has_side_effects=True, vmem_limit_bytes=55000 * 1024
        ),
    )(
        stored_grads.reshape(K, K),
        inverse_fisher.reshape(K, K),
        query_grads.reshape(128, K),
        jnp.concatenate([example_row, query_slot.reshape(1, K)], axis=0),
    )
    return total * (1.0 / math.sqrt(K * 32))


def solution(mesh):
    split = Mesh(mesh.devices.reshape(tuple(SIZE[a] for a in AXES)), AXES)
    placed = (P(AXES, None, None), P(LAY, None, None), P(GRP, LAY, None), P(GRP, None), P())
    return jax.shard_map(body, mesh=split, in_specs=placed, out_specs=P(AXES, None), check_vma=False)
```

```python
import math

import jax
import jax.numpy as jnp
from jax import lax
from jax.experimental import pallas as pl
from jax.experimental.pallas import tpu as pltpu
from jax.sharding import Mesh
from jax.sharding import PartitionSpec as P

AXES = ("y", "xl", "xh", "z", "c")
SIZE = {"y": 4, "xl": 2, "xh": 2, "z": 8, "c": 2}
GRP = ("y", "xl")
LAY = ("xh", "z", "c")
EPS = 1e-06
K = 1024
ROWS = 32
BF16 = jnp.bfloat16
F32 = jnp.float32
IN_Z = [(a, b) for a in range(2) for b in range(2)]
EARLY = 2
AHEAD = 5
FAR_FIRST = (4, 3, 5, 2, 6, 1, 7, 0)


def step_of(g):
    step = 0
    for i, d in enumerate((0, 3, 5, 4, 2, 6, 1, 7)):
        step = jnp.where(g == i, d, step)
    return step


def kernel(
    x_hbm, f_hbm, q_hbm, order_ref, out_ref,
    x_v, f_v, fh, fl, q_all, qpt, sendbuf, grads, normed, own, other, pick, col, acc,
    xs, xr, zs, zr,
    in_sem, q_send, q_recv, a_send, a_recv, e_send, e_recv, x_send, x_recv, z_send, z_recv,
):
    me = {a: lax.axis_index(a) for a in AXES}
    z, c, xh = me["z"], me["c"], me["xh"]

    def shifted(**off):
        return tuple(lax.rem(me[a] + off.get(a, 0), SIZE[a]) for a in AXES)

    def remote(src, dst, ssem, rsem, dev):
        return pltpu.make_async_remote_copy(
            src_ref=src, dst_ref=dst, send_sem=ssem, recv_sem=rsem,
            device_id=dev, device_id_type=pl.DeviceIdType.MESH,
        )

    load_x = pltpu.make_async_copy(x_hbm, x_v, in_sem.at[0])
    load_f = pltpu.make_async_copy(f_hbm, f_v, in_sem.at[1])
    grp_me = me["y"] * 2 + me["xl"]
    my_q = pl.ds(pl.multiple_of(grp_me * 128, 128), 128)
    load_q = pltpu.make_async_copy(q_hbm, q_all.at[my_q], in_sem.at[2])
    load_x.start()

    barrier = pltpu.get_barrier_semaphore()
    lay_peers = [(a, b, d) for a in range(2) for b in range(8) for d in range(2) if (a, b, d) != (0, 0, 0)]
    grp_peers = [(0, 1), (1, 0), (2, 0), (3, 0)]
    lay_peers.sort(key=lambda p: -(2 * p[0] + min(p[1], 8 - p[1])))
    for a, b, d in lay_peers:
        pl.semaphore_signal(barrier, inc=1, device_id=shifted(xh=a, z=b, c=d), device_id_type=pl.DeviceIdType.MESH)
    for a, b in grp_peers:
        pl.semaphore_signal(barrier, inc=1, device_id=shifted(y=a, xl=b), device_id_type=pl.DeviceIdType.MESH)
    load_f.start()
    load_q.start()
    row_in = lax.broadcasted_iota(jnp.int32, (128, K), 0)
    col_in = lax.broadcasted_iota(jnp.int32, (128, K), 1)
    source = lax.rem(row_in, 32) * 32 + (row_in // 64) * 16 + lax.rem(row_in // 32, 2)
    base = source - col_in
    slot = pl.multiple_of(xh * 64 + c * 32, 32)

    def a_copy(g, q, sending):
        d = step_of(g)
        a, b = IN_Z[q]
        if sending:
            to = (me["y"], me["xl"], lax.rem(xh + a, 2), lax.rem(z + d, 8), lax.rem(c + b, 2))
            rows = pl.multiple_of(to[2] * 64 + to[4] * 32, 32)
            src, dst = sendbuf.at[g, pl.ds(rows, 32)], grads.at[z, pl.ds(slot, 32)]
        else:
            to = (me["y"], me["xl"], lax.rem(xh + a, 2), lax.rem(z + 8 - d, 8), lax.rem(c + b, 2))
            rows = pl.multiple_of(to[2] * 64 + to[4] * 32, 32)
            src, dst = sendbuf.at[g, pl.ds(rows, 32)], grads.at[to[3], pl.ds(rows, 32)]
        return remote(src, dst, a_send.at[g, q], a_recv.at[g, q], to)

    def prepare(g):
        to_z = lax.rem(z + step_of(g), 8)
        mask = jnp.where(base + 2 * to_z == 0, 1.0, 0.0).astype(BF16)
        sendbuf[g] = jnp.dot(mask, x_v[...], preferred_element_type=F32).astype(BF16)

    def prepare_next(g, carry):
        prepare(g)
        return carry

    def send(g):
        for q in (2, 3, 0, 1):
            a_copy(g, q, True).start()

    def prepare_and_send(g, carry):
        prepare(g)
        send(g)
        return carry

    load_x.wait()
    lax.fori_loop(0, 2, prepare_next, 0)
    pl.semaphore_wait(barrier, len(lay_peers) + len(grp_peers))

    def q_rows(y, xl):
        return pl.ds(pl.multiple_of((y * 2 + xl) * 128, 128), 128)

    def q_copy(i, sending):
        a = 0 if i == 0 else (i - 1) % 3 + 1
        b = 1 if i == 0 else 0
        if sending:
            rows = q_rows(me["y"], me["xl"] if i < 4 else 1 - me["xl"])
            src = q_hbm if i < 4 else q_all.at[rows]
            to = shifted(y=a, xl=b)
        else:
            to = shifted(y=4 - a, xl=b)
            rows = q_rows(to[0], to[1] if i < 4 else 1 - to[1])
            src = q_hbm
        return remote(src, q_all.at[rows], q_send.at[i], q_recv.at[i], to)

    for i in range(4):
        q_copy(i, True).start()
    send(1)
    for q in range(1, 4):
        a_copy(0, q, True).start()
    lax.fori_loop(2, AHEAD + 1, prepare_and_send, 0)
    lax.fori_loop(AHEAD + 1, 8, prepare_next, 0)
    grads[z, pl.ds(slot, 32)] = sendbuf[0, pl.ds(slot, 32)]

    load_f.wait()

    def split(i, carry):
        rows = pl.ds(pl.multiple_of(i * 128, 128), 128)
        f = f_v[rows, :]
        hi = f.astype(BF16)
        fh[rows, :] = hi
        fl[rows, :] = (f - hi.astype(F32)).astype(BF16)
        return carry

    lax.fori_loop(0, 8, split, 0)

    q_copy(0, False).wait_recv()
    for i in range(4, 7):
        q_copy(i, True).start()

    diagonal = lax.broadcasted_iota(jnp.int32, (128, 128), 0) == lax.broadcasted_iota(jnp.int32, (128, 128), 1)

    def as_column(which, i):
        lanes = pl.ds(pl.multiple_of(i * 128, 128), 128)
        row = jnp.broadcast_to(order_ref[pl.ds(which, 1), lanes].astype(F32), (128, 128))
        return jnp.sum(jnp.where(diagonal, row, 0.0), axis=1, keepdims=True)

    def columns(i, carry):
        rows = pl.ds(pl.multiple_of(i * 128, 128), 128)
        col[rows, :] = jnp.broadcast_to(as_column(0, i), (128, 128))
        return carry

    lax.fori_loop(0, 8, columns, 0)

    lane = lax.broadcasted_iota(jnp.int32, (32, 128), 1)
    stored = ((lane // 64) * 512 + lax.rem(lane, 64)).astype(F32)

    def picks(i, carry):
        to_z, to_xh = i // 2, lax.rem(i, 2)
        wanted = col[pl.ds(pl.multiple_of(to_xh * 512 + to_z * 64 + c * 32, 32), 32), :] - stored
        rows = pl.ds(pl.multiple_of(i * 32, 32), 32)
        for zg in range(8):
            pick[zg, rows, :] = jnp.where(wanted == float(zg * 64), 1.0, 0.0).astype(BF16)
        return carry

    lax.fori_loop(0, 16, picks, 0)
    acc[...] = jnp.zeros_like(acc)

    def source_z(g):
        return lax.rem(z + 8 - step_of(g), 8)

    def arrived(g):
        for q in range(4):
            a_copy(g, q, True).wait_send()

        @pl.when(g + AHEAD < 8)
        def _():
            send(g + AHEAD)

        for q in range(4):
            a_copy(g, q, False).wait_recv()

    def normalise(g):
        at = source_z(g)
        rows = grads[at]
        pre = jnp.dot(rows, fh[...], preferred_element_type=F32) + jnp.dot(rows, fl[...], preferred_element_type=F32)
        mean_square = jnp.mean(pre * pre, axis=1, keepdims=True) + EPS
        normed[at] = (pre * lax.rsqrt(mean_square)).astype(BF16)

    def normalise_next(g, carry):
        arrived(g)
        normalise(g)
        return carry

    for q in range(1, 4):
        a_copy(0, q, False).wait_recv()
    normalise(0)
    lax.fori_loop(1, EARLY, normalise_next, 0)

    load_q.wait()
    for i in range(1, 7):
        q_copy(i, False).wait_recv()
    lanes_f = lax.broadcasted_iota(jnp.int32, (128, K), 1).astype(F32)

    def ask(i, carry):
        mask = jnp.where(as_column(1, i) == lanes_f, 1.0, 0.0).astype(BF16)
        chosen = jnp.dot(mask, q_all[...], preferred_element_type=F32)
        lanes = pl.ds(pl.multiple_of(i * 128, 128), 128)
        qpt[:, lanes] = jnp.transpose(chosen).astype(BF16)
        return carry

    lax.fori_loop(0, 8, ask, 0)

    def exchange(g):
        at = source_z(g)
        return remote(own.at[at], other.at[at], e_send.at[g], e_recv.at[g], shifted(c=1))

    def score(g):
        at = source_z(g)
        own[at] = jnp.dot(normed[at], qpt[...], preferred_element_type=F32)
        exchange(g).start()

    def collect(g):
        exchange(g).wait_recv()
        at = source_z(g)
        both = (own[at] + other[at]).astype(BF16)
        acc[...] += jnp.dot(pick[at], both, preferred_element_type=F32)

    score(0)

    def score_early(g, carry):
        score(g)
        return carry

    lax.fori_loop(1, EARLY, score_early, 0)

    def score_late(g, carry):
        arrived(g)
        normalise(g)
        score(g)
        collect(g - 2)
        return carry

    lax.fori_loop(EARLY, 8, score_late, 0)
    collect(6)
    collect(7)

    def piece(k, to_xh):
        to_z = lax.rem(z + FAR_FIRST[k], 8)
        return acc[pl.ds(pl.multiple_of(to_z * 64 + to_xh * 32, 32), 32), :]

    def x_copy(k):
        return remote(xs.at[k], xr.at[k], x_send.at[k], x_recv.at[k], shifted(xh=1))

    def z_copy(k):
        return remote(zs.at[k], zr.at[k], z_send.at[k], z_recv.at[k], shifted(z=FAR_FIRST[k]))

    for k in range(8):
        xs[k] = piece(k, 1 - xh).astype(BF16)
        x_copy(k).start()
    for k in range(7):
        x_copy(k).wait_recv()
        zs[k] = (piece(k, xh) + xr[k].astype(F32)).astype(BF16)
        z_copy(k).start()
    x_copy(7).wait_recv()
    total = piece(7, xh) + xr[7].astype(F32)
    for k in range(6, -1, -1):
        z_copy(k).wait_recv()
        total = total + zr[k].astype(F32)
    out_ref[...] = total

    for i in range(7):
        q_copy(i, True).wait_send()
    for q in range(1, 4):
        a_copy(0, q, True).wait_send()

    def drain(g, carry):
        exchange(g).wait_send()
        return carry

    lax.fori_loop(1, 8, drain, 0)
    exchange(0).wait_send()
    for k in range(8):
        x_copy(k).wait_send()
        if k < 7:
            z_copy(k).wait_send()


def body(stored_grads, inverse_fisher, query_grads, example_row, query_slot):
    dma = pltpu.SemaphoreType.DMA
    hbm = pl.BlockSpec(memory_space=pltpu.HBM)
    vmem = pl.BlockSpec(memory_space=pltpu.VMEM)
    total = pl.pallas_call(
        kernel,
        out_shape=jax.ShapeDtypeStruct((ROWS, K), F32),
        in_specs=[hbm, hbm, hbm, vmem],
        out_specs=vmem,
        scratch_shapes=[
            pltpu.VMEM((K, K), BF16),
            pltpu.VMEM((K, K), F32),
            pltpu.VMEM((K, K), BF16),
            pltpu.VMEM((K, K), BF16),
            pltpu.VMEM((K, K), BF16),
            pltpu.VMEM((K, K), BF16),
            pltpu.VMEM((8, 128, K), BF16),
            pltpu.VMEM((8, 128, K), BF16),
            pltpu.VMEM((8, 128, K), BF16),
            pltpu.VMEM((8, 128, K), F32),
            pltpu.VMEM((8, 128, K), F32),
            pltpu.VMEM((8, 512, 128), BF16),
            pltpu.VMEM((K, 128), F32),
            pltpu.VMEM((512, K), F32),
            pltpu.VMEM((8, ROWS, K), BF16),
            pltpu.VMEM((8, ROWS, K), BF16),
            pltpu.VMEM((8, ROWS, K), BF16),
            pltpu.VMEM((8, ROWS, K), BF16),
            dma((3,)), dma((7,)), dma((7,)), dma((8, 4)), dma((8, 4)), dma((8,)), dma((8,)),
            dma((8,)), dma((8,)), dma((8,)), dma((8,)),
        ],
        name="attribution",
        compiler_params=pltpu.CompilerParams(
            collective_id=0, has_side_effects=True, vmem_limit_bytes=55000 * 1024
        ),
    )(
        stored_grads.reshape(K, K),
        inverse_fisher.reshape(K, K),
        query_grads.reshape(128, K),
        jnp.concatenate([example_row, query_slot.reshape(1, K)], axis=0),
    )
    return total * (1.0 / math.sqrt(K * 32))


def solution(mesh):
    split = Mesh(mesh.devices.reshape(tuple(SIZE[a] for a in AXES)), AXES)
    placed = (P(AXES, None, None), P(LAY, None, None), P(GRP, LAY, None), P(GRP, None), P())
    return jax.shard_map(body, mesh=split, in_specs=placed, out_specs=P(AXES, None), check_vma=False)
```

```python
import math

import jax
import jax.numpy as jnp
from jax import lax
from jax.experimental import pallas as pl
from jax.experimental.pallas import tpu as pltpu
from jax.sharding import Mesh
from jax.sharding import PartitionSpec as P

AXES = ("y", "xl", "xh", "z", "c")
SIZE = {"y": 4, "xl": 2, "xh": 2, "z": 8, "c": 2}
GRP = ("y", "xl")
LAY = ("xh", "z", "c")
EPS = 1e-06
K = 1024
ROWS = 32
BF16 = jnp.bfloat16
F32 = jnp.float32
IN_Z = [(a, b) for a in range(2) for b in range(2)]
EARLY = 2
AHEAD = 5
FAR_FIRST = (4, 3, 5, 2, 6, 1, 7, 0)


def step_of(g):
    step = 0
    for i, d in enumerate((0, 3, 5, 4, 2, 6, 1, 7)):
        step = jnp.where(g == i, d, step)
    return step


def kernel(
    x_hbm, f_hbm, q_hbm, order_ref, out_ref,
    x_v, f_v, fh, fl, q_all, qpt, sendbuf, grads, normed, own, other, pick, col, acc,
    xs, xr, zs, zr,
    in_sem, q_send, q_recv, a_send, a_recv, e_send, e_recv, x_send, x_recv, z_send, z_recv,
):
    me = {a: lax.axis_index(a) for a in AXES}
    z, c, xh = me["z"], me["c"], me["xh"]

    def shifted(**off):
        return tuple(lax.rem(me[a] + off.get(a, 0), SIZE[a]) for a in AXES)

    def remote(src, dst, ssem, rsem, dev):
        return pltpu.make_async_remote_copy(
            src_ref=src, dst_ref=dst, send_sem=ssem, recv_sem=rsem,
            device_id=dev, device_id_type=pl.DeviceIdType.MESH,
        )

    load_x = pltpu.make_async_copy(x_hbm, x_v, in_sem.at[0])
    load_f = pltpu.make_async_copy(f_hbm, f_v, in_sem.at[1])
    grp_me = me["y"] * 2 + me["xl"]
    my_q = pl.ds(pl.multiple_of(grp_me * 128, 128), 128)
    load_q = pltpu.make_async_copy(q_hbm, q_all.at[my_q], in_sem.at[2])
    load_x.start()

    barrier = pltpu.get_barrier_semaphore()
    lay_peers = [(a, b, d) for a in range(2) for b in range(8) for d in range(2) if (a, b, d) != (0, 0, 0)]
    grp_peers = [(0, 1), (1, 0), (2, 0), (3, 0)]
    lay_peers.sort(key=lambda p: -(2 * p[0] + min(p[1], 8 - p[1])))
    for a, b, d in lay_peers:
        pl.semaphore_signal(barrier, inc=1, device_id=shifted(xh=a, z=b, c=d), device_id_type=pl.DeviceIdType.MESH)
    for a, b in grp_peers:
        pl.semaphore_signal(barrier, inc=1, device_id=shifted(y=a, xl=b), device_id_type=pl.DeviceIdType.MESH)
    load_f.start()
    load_q.start()
    row_in = lax.broadcasted_iota(jnp.int32, (128, K), 0)
    col_in = lax.broadcasted_iota(jnp.int32, (128, K), 1)
    source = lax.rem(row_in, 32) * 32 + (row_in // 64) * 16 + lax.rem(row_in // 32, 2)
    base = source - col_in
    slot = pl.multiple_of(xh * 64 + c * 32, 32)

    def a_copy(g, q, sending):
        d = step_of(g)
        a, b = IN_Z[q]
        if sending:
            to = (me["y"], me["xl"], lax.rem(xh + a, 2), lax.rem(z + d, 8), lax.rem(c + b, 2))
            rows = pl.multiple_of(to[2] * 64 + to[4] * 32, 32)
            src, dst = sendbuf.at[g, pl.ds(rows, 32)], grads.at[z, pl.ds(slot, 32)]
        else:
            to = (me["y"], me["xl"], lax.rem(xh + a, 2), lax.rem(z + 8 - d, 8), lax.rem(c + b, 2))
            rows = pl.multiple_of(to[2] * 64 + to[4] * 32, 32)
            src, dst = sendbuf.at[g, pl.ds(rows, 32)], grads.at[to[3], pl.ds(rows, 32)]
        return remote(src, dst, a_send.at[g, q], a_recv.at[g, q], to)

    def prepare(g):
        to_z = lax.rem(z + step_of(g), 8)
        mask = jnp.where(base + 2 * to_z == 0, 1.0, 0.0).astype(BF16)
        sendbuf[g] = jnp.dot(mask, x_v[...], preferred_element_type=F32).astype(BF16)

    def prepare_next(g, carry):
        prepare(g)
        return carry

    def send(g):
        for q in (2, 3, 0, 1):
            a_copy(g, q, True).start()

    def prepare_and_send(g, carry):
        prepare(g)
        send(g)
        return carry

    load_x.wait()
    lax.fori_loop(0, 2, prepare_next, 0)
    pl.semaphore_wait(barrier, len(lay_peers) + len(grp_peers))

    def q_rows(y, xl):
        return pl.ds(pl.multiple_of((y * 2 + xl) * 128, 128), 128)

    def q_copy(i, sending):
        a = 0 if i == 0 else (i - 1) % 3 + 1
        b = 1 if i == 0 else 0
        if sending:
            rows = q_rows(me["y"], me["xl"] if i < 4 else 1 - me["xl"])
            src = q_hbm if i < 4 else q_all.at[rows]
            to = shifted(y=a, xl=b)
        else:
            to = shifted(y=4 - a, xl=b)
            rows = q_rows(to[0], to[1] if i < 4 else 1 - to[1])
            src = q_hbm
        return remote(src, q_all.at[rows], q_send.at[i], q_recv.at[i], to)

    for i in range(4):
        q_copy(i, True).start()
    send(1)
    for q in range(1, 4):
        a_copy(0, q, True).start()
    lax.fori_loop(2, AHEAD + 1, prepare_and_send, 0)
    lax.fori_loop(AHEAD + 1, 8, prepare_next, 0)
    grads[z, pl.ds(slot, 32)] = sendbuf[0, pl.ds(slot, 32)]

    load_f.wait()

    def split(i, carry):
        rows = pl.ds(pl.multiple_of(i * 128, 128), 128)
        f = f_v[rows, :]
        hi = f.astype(BF16)
        fh[rows, :] = hi
        fl[rows, :] = (f - hi.astype(F32)).astype(BF16)
        return carry

    lax.fori_loop(0, 8, split, 0)

    q_copy(0, False).wait_recv()
    for i in range(4, 7):
        q_copy(i, True).start()

    diagonal = lax.broadcasted_iota(jnp.int32, (128, 128), 0) == lax.broadcasted_iota(jnp.int32, (128, 128), 1)

    def as_column(which, i):
        lanes = pl.ds(pl.multiple_of(i * 128, 128), 128)
        row = jnp.broadcast_to(order_ref[pl.ds(which, 1), lanes].astype(F32), (128, 128))
        return jnp.sum(jnp.where(diagonal, row, 0.0), axis=1, keepdims=True)

    def columns(i, carry):
        rows = pl.ds(pl.multiple_of(i * 128, 128), 128)
        col[rows, :] = jnp.broadcast_to(as_column(0, i), (128, 128))
        return carry

    lax.fori_loop(0, 8, columns, 0)

    lane = lax.broadcasted_iota(jnp.int32, (32, 128), 1)
    stored = ((lane // 64) * 512 + lax.rem(lane, 64)).astype(F32)

    def picks(i, carry):
        to_z, to_xh = i // 2, lax.rem(i, 2)
        wanted = col[pl.ds(pl.multiple_of(to_xh * 512 + to_z * 64 + c * 32, 32), 32), :] - stored
        rows = pl.ds(pl.multiple_of(i * 32, 32), 32)
        for zg in range(8):
            pick[zg, rows, :] = jnp.where(wanted == float(zg * 64), 1.0, 0.0).astype(BF16)
        return carry

    lax.fori_loop(0, 16, picks, 0)
    acc[...] = jnp.zeros_like(acc)

    def source_z(g):
        return lax.rem(z + 8 - step_of(g), 8)

    def arrived(g):
        for q in range(4):
            a_copy(g, q, True).wait_send()

        @pl.when(g + AHEAD < 8)
        def _():
            send(g + AHEAD)

        for q in range(4):
            a_copy(g, q, False).wait_recv()

    def normalise(g):
        at = source_z(g)
        rows = grads[at]
        pre = jnp.dot(rows, fh[...], preferred_element_type=F32) + jnp.dot(rows, fl[...], preferred_element_type=F32)
        mean_square = jnp.mean(pre * pre, axis=1, keepdims=True) + EPS
        normed[at] = (pre * lax.rsqrt(mean_square)).astype(BF16)

    def normalise_next(g, carry):
        arrived(g)
        normalise(g)
        return carry

    for q in range(1, 4):
        a_copy(0, q, False).wait_recv()
    normalise(0)
    lax.fori_loop(1, EARLY, normalise_next, 0)

    load_q.wait()
    for i in range(1, 7):
        q_copy(i, False).wait_recv()
    lanes_f = lax.broadcasted_iota(jnp.int32, (128, K), 1).astype(F32)

    def ask(i, carry):
        mask = jnp.where(as_column(1, i) == lanes_f, 1.0, 0.0).astype(BF16)
        chosen = jnp.dot(mask, q_all[...], preferred_element_type=F32)
        lanes = pl.ds(pl.multiple_of(i * 128, 128), 128)
        qpt[:, lanes] = jnp.transpose(chosen).astype(BF16)
        return carry

    lax.fori_loop(0, 8, ask, 0)

    def exchange(g):
        at = source_z(g)
        return remote(own.at[at], other.at[at], e_send.at[g], e_recv.at[g], shifted(c=1))

    def score(g):
        at = source_z(g)
        own[at] = jnp.dot(normed[at], qpt[...], preferred_element_type=F32)
        exchange(g).start()

    def collect(g):
        exchange(g).wait_recv()
        at = source_z(g)
        both = (own[at] + other[at]).astype(BF16)
        acc[...] += jnp.dot(pick[at], both, preferred_element_type=F32)

    score(0)

    def score_early(g, carry):
        score(g)
        collect(g - 1)
        return carry

    lax.fori_loop(1, EARLY, score_early, 0)

    def score_late(g, carry):
        arrived(g)
        normalise(g)
        score(g)
        collect(g - 1)
        return carry

    lax.fori_loop(EARLY, 8, score_late, 0)
    collect(7)

    def piece(k, to_xh):
        to_z = lax.rem(z + FAR_FIRST[k], 8)
        return acc[pl.ds(pl.multiple_of(to_z * 64 + to_xh * 32, 32), 32), :]

    def x_copy(k):
        return remote(xs.at[k], xr.at[k], x_send.at[k], x_recv.at[k], shifted(xh=1))

    def z_copy(k):
        return remote(zs.at[k], zr.at[k], z_send.at[k], z_recv.at[k], shifted(z=FAR_FIRST[k]))

    for k in range(8):
        xs[k] = piece(k, 1 - xh).astype(BF16)
        x_copy(k).start()
    for k in range(7):
        x_copy(k).wait_recv()
        zs[k] = (piece(k, xh) + xr[k].astype(F32)).astype(BF16)
        z_copy(k).start()
    x_copy(7).wait_recv()
    total = piece(7, xh) + xr[7].astype(F32)
    for k in range(6, -1, -1):
        z_copy(k).wait_recv()
        total = total + zr[k].astype(F32)
    out_ref[...] = total

    for i in range(7):
        q_copy(i, True).wait_send()
    for q in range(1, 4):
        a_copy(0, q, True).wait_send()

    def drain(g, carry):
        exchange(g).wait_send()
        return carry

    lax.fori_loop(1, 8, drain, 0)
    exchange(0).wait_send()
    for k in range(8):
        x_copy(k).wait_send()
        if k < 7:
            z_copy(k).wait_send()


def body(stored_grads, inverse_fisher, query_grads, example_row, query_slot):
    dma = pltpu.SemaphoreType.DMA
    hbm = pl.BlockSpec(memory_space=pltpu.HBM)
    vmem = pl.BlockSpec(memory_space=pltpu.VMEM)
    total = pl.pallas_call(
        kernel,
        out_shape=jax.ShapeDtypeStruct((ROWS, K), F32),
        in_specs=[hbm, hbm, hbm, vmem],
        out_specs=vmem,
        scratch_shapes=[
            pltpu.VMEM((K, K), BF16),
            pltpu.VMEM((K, K), F32),
            pltpu.VMEM((K, K), BF16),
            pltpu.VMEM((K, K), BF16),
            pltpu.VMEM((K, K), BF16),
            pltpu.VMEM((K, K), BF16),
            pltpu.VMEM((8, 128, K), BF16),
            pltpu.VMEM((8, 128, K), BF16),
            pltpu.VMEM((8, 128, K), BF16),
            pltpu.VMEM((8, 128, K), F32),
            pltpu.VMEM((8, 128, K), F32),
            pltpu.VMEM((8, 512, 128), BF16),
            pltpu.VMEM((K, 128), F32),
            pltpu.VMEM((512, K), F32),
            pltpu.VMEM((8, ROWS, K), BF16),
            pltpu.VMEM((8, ROWS, K), BF16),
            pltpu.VMEM((8, ROWS, K), BF16),
            pltpu.VMEM((8, ROWS, K), BF16),
            dma((3,)), dma((7,)), dma((7,)), dma((8, 4)), dma((8, 4)), dma((8,)), dma((8,)),
            dma((8,)), dma((8,)), dma((8,)), dma((8,)),
        ],
        name="attribution",
        compiler_params=pltpu.CompilerParams(
            collective_id=0, has_side_effects=True, vmem_limit_bytes=55000 * 1024
        ),
    )(
        stored_grads.reshape(K, K),
        inverse_fisher.reshape(K, K),
        query_grads.reshape(128, K),
        jnp.concatenate([example_row, query_slot.reshape(1, K)], axis=0),
    )
    return total * (1.0 / math.sqrt(K * 32))


def solution(mesh):
    split = Mesh(mesh.devices.reshape(tuple(SIZE[a] for a in AXES)), AXES)
    placed = (P(AXES, None, None), P(LAY, None, None), P(GRP, LAY, None), P(GRP, None), P())
    return jax.shard_map(body, mesh=split, in_specs=placed, out_specs=P(AXES, None), check_vma=False)
```
